256 devices in a mesh: tm: 64 (over z, x, y_lo), gz: 4 (over y_hi, core).
Axes of the slice: x: 4, y: 4 (y_hi: 2, y_lo: 2; y = y_hi * 2 + y_lo), z: 8, core: 2. Of those that a mesh axis runs over, the one named last changes fastest.
Arguments:
- source: float32 [128, 32, 32, 512], P('tm', None, None, 'gz'), may hold values from -8 to 8
- initial_guess: float32 [128, 32, 32, 512], P('tm', None, None, 'gz'), may hold values from -8 to 8
- diffusivity: float32 [32, 32, 512], P(None, None, 'gz'), may hold values from 0.25 to 2.5
Outputs:
- solution: float32 [128, 32, 32, 512], P('tm', None, None, 'gz')
- residual: float32 [128, 32, 32, 512], P('tm', None, None, 'gz')
The draws below stay inside these ranges and needn't reach their ends.
All inputs are finite; a program needn't handle non-finite values.
Results may differ from the reference program's by a relative error of at most 0.00002.
Values sent between devices are 32-bit elements; how exact they have to be, the bound alone decides.
No kernel may reach another device: no remote copies, remote signals or barrier semaphores. Data moves between devices by JAX's collectives and lax.ppermute only.
A program may use at most 128 MiB of HBM per device.

```python
import math
import jax
import jax.numpy as jnp

NX = 32
NY = 32
LEVELS = 5
SWEEPS = 2
CSWEEPS = 4
NT = 128
NZ = 512


def level_of(own_key, extent, pieces, smallest, largest):
    gain = 1.0
    for axis_at, shards_of in pieces:
        steps = jax.random.uniform(jax.random.fold_in(jax.random.fold_in(own_key, 6), axis_at), (shards_of,), jnp.float32, smallest / len(pieces), largest / len(pieces))
        gain = gain * jnp.repeat(jnp.exp(steps), extent[axis_at] // shards_of).reshape((-1,) + (1,) * (len(extent) - 1 - axis_at))
    return gain


def noise(key, extent, spread, reach, pieces=(), dtype=jnp.bfloat16):
    entries = jax.random.normal(key, extent, jnp.float32) * spread
    if len(pieces) > 0:
        entries = level_of(key, extent, pieces, -0.22, 0.18) * entries
    return jnp.clip(entries, min=-reach, max=reach).astype(dtype)


def setup_inputs(seed: int = 0) -> dict:
    streams_of = jax.random.split(jax.random.key(seed), 4)
    source = noise(streams_of[0], (NT, NX, NY, NZ), 1.0, 8.0, ((0, 64), (3, 4)), jnp.float32)
    initial_guess = noise(streams_of[1], (NT, NX, NY, NZ), 1.0, 8.0, ((0, 64), (3, 4)), jnp.float32)
    diffusivity = jnp.clip(jnp.exp(math.log(2.5) - 2.3025851 * jax.random.uniform(streams_of[2], (NX, NY, NZ), jnp.float32) ** level_of(streams_of[2], (NX, NY, NZ), ((2, 4),), -0.2, 0.2)), 0.25, 2.5)
    return dict(source=source, initial_guess=initial_guess, diffusivity=diffusivity)


damping = 0.8
base_coef = 8.0


def operate(values, diffusivity, time_coef):
    before = jnp.concatenate([jnp.zeros_like(values[:1]), values[:-1]], axis=0)
    padded = jnp.pad(values, ((0, 0), (1, 1), (1, 1), (1, 1)))
    beside = padded[:, 2:, 1:-1, 1:-1] + padded[:, :-2, 1:-1, 1:-1]
    beside = beside + padded[:, 1:-1, 2:, 1:-1] + padded[:, 1:-1, :-2, 1:-1]
    beside = beside + padded[:, 1:-1, 1:-1, 2:] + padded[:, 1:-1, 1:-1, :-2]
    return time_coef * (values - before) + diffusivity * (6.0 * values - beside)


def smooth(values, target, diffusivity, time_coef, sweep_count):
    scaled = damping / (time_coef + 6.0 * diffusivity)
    for sweep_num in range(sweep_count):
        values = values + scaled * (target - operate(values, diffusivity, time_coef))
    return values


def cycle(level_num, values, target, diffusivity):
    time_coef = base_coef / (2.0 ** level_num)
    if level_num == LEVELS - 1:
        return smooth(values, target, diffusivity, time_coef, CSWEEPS)
    values = smooth(values, target, diffusivity, time_coef, SWEEPS)
    leftover = target - operate(values, diffusivity, time_coef)
    coarse_res = (leftover[0::2] + leftover[1::2]) * 0.5
    correction = cycle(level_num + 1, jnp.zeros_like(coarse_res), coarse_res, diffusivity)
    values = values + jnp.repeat(correction, 2, axis=0)
    return smooth(values, target, diffusivity, time_coef, SWEEPS)


def reference(source, initial_guess, diffusivity):
    solution = cycle(0, initial_guess, source, diffusivity)
    residual = source - operate(solution, diffusivity, base_coef)
    return solution, residual
```

```python
import functools
import math
import jax
import jax.numpy as jnp
from jax import lax
from jax.experimental import pallas as pl
from jax.experimental.pallas import tpu as pltpu
from jax.sharding import PartitionSpec as P

damping = 0.8
keep = 1.0 - 0.8
base_coef = 8.0

SIDE = 32
OWN = 128
HALO = 22
EXT = OWN + 2 * HALO
GROUP = 8
PIECE = 17
WIDE = PIECE + 30
COARSE = GROUP * PIECE + 30
LOW = HALO - 19
F32 = jnp.float32

VM = pl.BlockSpec(memory_space=pltpu.VMEM)
SM = pl.BlockSpec(memory_space=pltpu.SMEM)


def call(body, outs, args, scratch=(), n_scalar=0):
    single = isinstance(outs, tuple)
    shapes = [outs] if single else list(outs)
    held = shapes + list(scratch) + [a.shape for a in args[n_scalar:]]
    need = sum(4 * math.prod(s) for s in held)
    result = pl.pallas_call(
        body,
        out_shape=[jax.ShapeDtypeStruct(s, F32) for s in shapes],
        in_specs=[SM] * n_scalar + [VM] * (len(args) - n_scalar),
        out_specs=[VM] * len(shapes),
        scratch_shapes=[pltpu.VMEM(s, F32) for s in scratch],
        compiler_params=pltpu.CompilerParams(vmem_limit_bytes=need + (2 << 20)),
    )(*args)
    return result[0] if single else result


def planes(low, high, width, fn):
    width = min(width, high - low)

    def step(i, carry):
        fn(pl.ds(jnp.minimum(low + i * width, high - width), width))
        return carry

    lax.fori_loop(0, -(-(high - low) // width), step, 0)


def width(steps):
    return max(1, 16 // steps)


def moved(at, by):
    return pl.ds(at.start + by, at.size)


def masks():
    lane = lax.broadcasted_iota(jnp.int32, (8, 128), 1)
    row = lax.broadcasted_iota(jnp.int32, (8, 128), 0)
    y = lane % SIDE
    return y != SIDE - 1, y != 0, lane < 96, lane >= 32, row < 7, row > 0


def beside(p, m):
    shape = p.shape
    p = p.reshape((-1,) + shape[-2:])
    y_up, y_down, x_in, x_out, row_up, row_down = [jnp.broadcast_to(a[None], p.shape) for a in m]
    zero = jnp.zeros_like(p)
    up = pltpu.roll(p, 96, 2)
    down = pltpu.roll(p, 32, 2)
    total = jnp.where(y_up, pltpu.roll(p, 127, 2), zero) + jnp.where(y_down, pltpu.roll(p, 1, 2), zero)
    total = total + jnp.where(x_in, up, jnp.where(row_up, pltpu.roll(up, 7, 1), zero))
    total = total + jnp.where(x_out, down, jnp.where(row_down, pltpu.roll(down, 1, 1), zero))
    return total.reshape(shape)


def spread(ref, t0, t1, z, m):
    p = ref[t0:t1, z]
    return p, beside(p, m) + ref[t0:t1, moved(z, -1)] + ref[t0:t1, moved(z, 1)]


def transposed_in(flag, v_ref, g_ref, d_ref, out, tail, edge_a, edge_b):
    for t in range(5):
        ref = v_ref if t < 2 else g_ref
        for s in range(8):
            rows = slice(s * 128, (s + 1) * 128)
            block = d_ref[rows, :] if t == 4 else ref[t % 2, rows, :]
            out[t, :, s, :] = block.T
            if t == 1:
                tail[0, :, s, :] = block.T
    odd = flag[0]
    far = OWN - HALO
    start_a = far * (1 - odd)
    start_b = far * odd

    def edge(z):
        edge_a[:, z] = out[:, moved(z, start_a)]
        edge_b[:, z] = out[:, moved(z, start_b)]

    planes(0, HALO, 2, edge)


def first_level(flag, own, edge_a, edge_b, back, back_edge, ext, v1, tail, prev):
    odd = flag[0]
    end = OWN + HALO
    at_a = end * (1 - odd)
    at_b = end * odd

    def centre(z):
        ext[0:5, moved(z, HALO)] = own[:, z]
        prev[0, moved(z, HALO)] = back[0, z]

    def edge(z):
        ext[0:5, moved(z, at_a)] = edge_a[:, z]
        ext[0:5, moved(z, at_b)] = edge_b[:, z]
        prev[0, moved(z, at_a)] = back_edge[0, z]
        prev[0, moved(z, at_b)] = back_edge[1, z]

    planes(0, OWN, 4, centre)
    planes(0, HALO, 2, edge)

    def scale(z):
        ext[5, z] = damping / (base_coef + 6.0 * ext[4, z])

    planes(0, EXT, 8, scale)
    pair_sweep(ext, ext, 0, prev, 0, v1, tail, 1, 1, EXT - 1)


def pair_sweep(ext, src, off, prev, off_prev, dst, tail, off_dst, low, high):
    m = masks()

    def fn(z):
        p, near = spread(src, 0, 2, moved(z, -off), m)
        before = jnp.concatenate([prev[0:1, moved(z, -off_prev)], p[0:1]], axis=0)
        value = keep * p + ext[5, z] * (ext[2:4, z] + base_coef * before + ext[4, z] * near)
        dst[:, moved(z, -off_dst)] = value
        tail[:, moved(z, -off_dst)] = value[1:2]

    planes(low, high, 8, fn)


def pair_left(ext, src, off, prev, off_prev, low, high, store):
    m = masks()

    def fn(z):
        p, near = spread(src, 0, 2, moved(z, -off), m)
        d = ext[4, z]
        before = jnp.concatenate([prev[0:1, moved(z, -off_prev)], p[0:1]], axis=0)
        store(z, ext[2:4, z] + base_coef * before + d * near - (base_coef + 6.0 * d) * p)

    planes(low, high, 8, fn)


def second_sweep(ext, v1, prev, v2, tail):
    pair_sweep(ext, v1, 1, prev, 1, v2, tail, 2, 2, EXT - 2)


def restrict_left(ext, v2, prev, out):
    def store(z, r):
        out[:, moved(z, -LOW)] = 0.5 * (r[0:1] + r[1:2])

    pair_left(ext, v2, 2, prev, 2, LOW, LOW + COARSE, store)


FIN = OWN + 2
FIRST = HALO - 1
E_LOW = HALO - 4


def third_sweep(ext, v2, prev, e0, e1, v3, tail, va, vp):
    def add(z):
        here = moved(z, -2)
        there = moved(z, -E_LOW)
        va[:, moved(z, -FIRST + 2)] = v2[:, here] + e0[:, there]
        vp[:, moved(z, -FIRST + 2)] = prev[:, here] + e1[:, there]

    planes(FIRST - 2, FIRST + FIN + 2, 8, add)
    pair_sweep(ext, va, FIRST - 2, vp, FIRST - 2, v3, tail, FIRST - 1, FIRST - 1, FIRST + FIN + 1)


def fourth_sweep(ext, v3, prev, v4, tail):
    pair_sweep(ext, v3, FIRST - 1, prev, FIRST - 1, v4, tail, FIRST, FIRST, FIRST + FIN)


def finish(ext, v4, prev, sol_out, res_out, res):
    def store(z, r):
        res[:, moved(z, -HALO)] = r

    for t in range(2):
        for s in range(8):
            sol_out[t, s * 128 : (s + 1) * 128, :] = v4[t, 1 : OWN + 1, s, :].T
    pair_left(ext, v4, FIRST, prev, FIRST, HALO, HALO + OWN, store)
    for t in range(2):
        for s in range(8):
            res_out[t, s * 128 : (s + 1) * 128, :] = res[t, :, s, :].T


def step_down(flag, d_ref, *refs, counts, own, c, low, last, tail_steps):
    history = refs[: len(counts)]
    g_own = refs[len(counts)]
    rest = refs[len(counts) + 1 :]
    past = sum(counts)
    total = past + own
    high = WIDE - low
    q = flag[0]
    if last:
        v_above, e_ref, tail, s_ref, g_ref, va, vb = rest
    elif tail_steps:
        v2, below, tail, s_ref, g_ref, va = rest
    else:
        v2, below, s_ref, g_ref, va = rest

    def gather(z):
        s = damping / (c + 6.0 * d_ref[z])
        s_ref[z] = s
        at = 0
        for i, (ref, n) in enumerate(zip(history, counts)):
            known = jnp.where(q > len(counts) - 1 - i, 1.0, 0.0).astype(F32)
            g = known * ref[:, moved(z, -low)]
            g_ref[at : at + n, z] = g
            va[at : at + n, z] = s * g
            at += n
        g = g_own[:, moved(z, -low)]
        g_ref[at:, z] = g
        va[at:, z] = s * g

    planes(low, high, width(total), gather)
    m = masks()

    def sweep(src, start, margin, store):
        def fn(z):
            p, near = spread(src, start, total, z, m)
            value = keep * p + s_ref[z] * (
                g_ref[start:total, z] + c * src[start - 1 : total - 1, z] + d_ref[z] * near
            )
            store(z, value)

        planes(low + margin, high - margin, width(total - start), fn)

    if last:

        def keep_b(z, value):
            vb[1:total, z] = value

        def keep_a(z, value):
            va[2:total, z] = value

        def keep_e(z, value):
            e_ref[:, moved(z, -low - 3)] = value
            tail[:, moved(z, -low - 3)] = v_above[v_above.shape[0] - 2 :, moved(z, 1 - low)] + value

        sweep(va, 1, 1, keep_b)
        sweep(vb, 2, 2, keep_a)
        sweep(va, 3, 3, keep_e)
        return

    def keep_v(z, value):
        v2[:, moved(z, -low - 1)] = value

    sweep(va, 1, 1, keep_v)

    def left(z):
        zz = moved(z, -low - 1)
        p, near = spread(v2, past - 1, total - 1, zz, m)
        d = d_ref[z]
        r = g_ref[past:total, z] + c * v2[past - 2 : total - 2, zz] + d * near - (c + 6.0 * d) * p
        for j in range(own // 2):
            value = 0.5 * (r[2 * j] + r[2 * j + 1])
            below[j, moved(z, -low - 2)] = value
            if tail_steps and j >= own // 2 - tail_steps:
                tail[j - own // 2 + tail_steps, moved(z, -low - 2)] = value

    planes(low + 2, high - 2, width(own), left)


def step_up(flag, d_ref, v2, g_last, g_own, v_last, e_own, *rest, own, c, low, e_low, top):
    if top:
        out, s_ref, va, vb = rest
    else:
        v_above, out, tail, s_ref, va, vb = rest
    q = flag[0]
    known = jnp.where(q > 0, 1.0, 0.0).astype(F32)
    n = own + 2
    last = g_last.shape[0] - 1

    def correct(z):
        s_ref[z] = damping / (c + 6.0 * d_ref[z])
        zz = moved(z, -low - 1)
        here = moved(z, -e_low)
        va[0:2, z] = known * v_last[:, here]
        for j in range(own // 2):
            e = e_own[j, here]
            va[2 + 2 * j, z] = v2[1 + 2 * j, zz] + e
            va[3 + 2 * j, z] = v2[2 + 2 * j, zz] + e

    planes(e_low, WIDE - e_low, width(n), correct)
    m = masks()

    def sweep1(z):
        p, near = spread(va, 1, n, z, m)
        g0 = known * g_last[last : last + 1, moved(z, -low)]
        g = jnp.concatenate([g0, g_own[:, moved(z, -low)]], axis=0)
        vb[:, z] = keep * p + s_ref[z] * (g + c * va[0 : n - 1, z] + d_ref[z] * near)

    planes(e_low + 1, WIDE - e_low - 1, width(n - 1), sweep1)

    def sweep2(z):
        p, near = spread(vb, 1, n - 1, z, m)
        value = keep * p + s_ref[z] * (
            g_own[:, moved(z, -low)] + c * vb[0 : n - 2, z] + d_ref[z] * near
        )
        here = moved(z, -e_low - 2)
        out[:, here] = value
        if not top:
            tail[:, here] = v_above[v_above.shape[0] - 2 :, moved(z, 1 - low)] + value[own - 1 :]

    planes(e_low + 2, WIDE - e_low - 2, width(own), sweep2)


def later(block, distance):
    count = lax.axis_size("tm")
    return lax.ppermute(block, "tm", [(i, i + distance) for i in range(count - distance)])


def around(block, distance):
    count = lax.axis_size("tm")
    return lax.ppermute(block, "tm", [(i, (i + distance) % count) for i in range(count)])


def body(source, initial_guess, diffusivity):
    T = (8, 128)
    slabs = lax.axis_size("gz")
    count = lax.axis_size("tm")
    odd = (lax.axis_index("gz") % 2).astype(jnp.int32).reshape(1)
    me = lax.axis_index("tm")
    q = (me // GROUP).astype(jnp.int32).reshape(1)
    piece = me % GROUP

    flat = lambda a: a.reshape(a.shape[:-3] + (SIDE * SIDE, OWN))
    own, tail, edge_a, edge_b = call(
        transposed_in,
        [(5, OWN) + T, (1, OWN) + T, (5, HALO) + T, (5, HALO) + T],
        (odd, flat(initial_guess), flat(source), flat(diffusivity)),
        n_scalar=1,
    )
    edge_a = lax.ppermute(edge_a, "gz", [(i, i ^ 1) for i in range(slabs)])
    pairs = [(i, i + 1) for i in range(1, slabs - 1, 2)]
    edge_b = lax.ppermute(edge_b, "gz", pairs + [(b, a) for a, b in pairs])
    prev = later(tail, 1)
    prev_edge = later(jnp.stack([edge_a[1], edge_b[1]]), 1)
    ext, v1, tail = call(
        first_level,
        [(6, EXT) + T, (2, EXT - 2) + T, (1, EXT - 2) + T],
        (odd, own, edge_a, edge_b, prev, prev_edge),
        scratch=[(1, EXT) + T],
        n_scalar=1,
    )
    v2, tail = call(second_sweep, [(2, EXT - 4) + T, (1, EXT - 4) + T], (ext, v1, later(tail, 1)))
    v2_prev = later(tail, 1)
    g1 = call(restrict_left, (1, COARSE) + T, (ext, v2, v2_prev))[0]

    groups = [list(range(a, a + GROUP)) for a in range(0, count, GROUP)]
    pieces = jnp.stack([g1[PIECE * b : PIECE * b + WIDE] for b in range(GROUP)])
    g = lax.all_to_all(pieces, "tm", 0, 0, axis_index_groups=groups, tiled=True)
    d = lax.dynamic_slice_in_dim(ext[4], LOW + PIECE * piece, WIDE, axis=0)

    saved = []
    own_steps = GROUP
    c = base_coef / 2.0
    low = 0
    g_tail = g[-2:]
    for level in range(1, 4):
        history = around(g_tail, GROUP)
        total = own_steps + 2
        wide = WIDE - 2 * low
        tail_steps = 2 if own_steps > 4 else 0
        v, g_below, *g_tail = call(
            functools.partial(
                step_down, counts=[2], own=own_steps, c=c, low=low, last=False, tail_steps=tail_steps
            ),
            [(total - 1, wide - 2) + T, (own_steps // 2, wide - 4) + T]
            + [(tail_steps, wide - 4) + T] * (tail_steps > 0),
            (q, d, history, g),
            scratch=[(WIDE,) + T, (total, WIDE) + T, (total, WIDE) + T],
            n_scalar=1,
        )
        g_tail = g_tail[0] if g_tail else g_below
        saved.append((v, history, g, own_steps, c, low))
        g = g_below
        own_steps //= 2
        c /= 2.0
        low += 2
    history = [around(g, i * GROUP) for i in (3, 2, 1)]
    wide = WIDE - 2 * low
    e, tail = call(
        functools.partial(
            step_down, counts=[1] * 3, own=1, c=c, low=low, last=True, tail_steps=0
        ),
        [(1, wide - 6) + T, (2, wide - 6) + T],
        (q, d, *history, g, saved[-1][0]),
        scratch=[(WIDE,) + T] + [(4, WIDE) + T] * 3,
        n_scalar=1,
    )
    e_low = low + 3
    while saved:
        v, g_last, g, own_steps, c, low = saved.pop()
        v_last = around(tail, GROUP)
        top = not saved
        narrow = WIDE - 2 * e_low - 4
        e = call(
            functools.partial(step_up, own=own_steps, c=c, low=low, e_low=e_low, top=top),
            [(own_steps, narrow) + T] + [(2, narrow) + T] * (not top),
            (q, d, v, g_last, g, v_last, e) + (() if top else (saved[-1][0],)),
            scratch=[(WIDE,) + T, (own_steps + 2, WIDE) + T, (own_steps + 1, WIDE) + T],
            n_scalar=1,
        )
        tail = e[-1]
        e = e[0]
        e_low += 2
    e0 = lax.all_to_all(e, "tm", 0, 0, axis_index_groups=groups, tiled=True)
    e0 = e0.reshape((1, GROUP * PIECE) + T)
    v3, tail = call(
        third_sweep,
        [(2, FIN + 2) + T, (1, FIN + 2) + T],
        (ext, v2, v2_prev, e0, later(e0, 1)),
        scratch=[(2, FIN + 4) + T, (1, FIN + 4) + T],
    )
    v4, tail = call(fourth_sweep, [(2, FIN) + T, (1, FIN) + T], (ext, v3, later(tail, 1)))
    sol, res = call(
        finish,
        [(2, SIDE * SIDE, OWN)] * 2,
        (ext, v4, later(tail, 1)),
        scratch=[(2, OWN) + T],
    )
    return sol.reshape(source.shape), res.reshape(source.shape)


def solution(mesh):
    placed = (P("tm", None, None, "gz"), P("tm", None, None, "gz"), P(None, None, "gz"))
    return jax.shard_map(
        body,
        mesh=mesh,
        in_specs=placed,
        out_specs=(P("tm", None, None, "gz"), P("tm", None, None, "gz")),
        check_vma=False,
    )
```

```python
import functools
import math
import jax
import jax.numpy as jnp
from jax import lax
from jax.experimental import pallas as pl
from jax.experimental.pallas import tpu as pltpu
from jax.sharding import PartitionSpec as P

damping = 0.8
keep = 1.0 - 0.8
base_coef = 8.0

SIDE = 32
OWN = 128
GROUP = 8
PIECE = OWN // GROUP
HALO = 15
WIDE = PIECE + 2 * HALO
F32 = jnp.float32

VM = pl.BlockSpec(memory_space=pltpu.VMEM)
SM = pl.BlockSpec(memory_space=pltpu.SMEM)


def call(body, outs, args, scratch=(), n_scalar=0):
    single = isinstance(outs, tuple)
    shapes = [outs] if single else list(outs)
    held = shapes + list(scratch) + [a.shape for a in args[n_scalar:]]
    need = sum(4 * math.prod(s) for s in held)
    result = pl.pallas_call(
        body,
        out_shape=[jax.ShapeDtypeStruct(s, F32) for s in shapes],
        in_specs=[SM] * n_scalar + [VM] * (len(args) - n_scalar),
        out_specs=[VM] * len(shapes),
        scratch_shapes=[pltpu.VMEM(s, F32) for s in scratch],
        compiler_params=pltpu.CompilerParams(vmem_limit_bytes=need + (2 << 20)),
    )(*args)
    return result[0] if single else result


def planes(low, high, width, fn):
    width = min(width, high - low)

    def step(i, carry):
        fn(pl.ds(jnp.minimum(low + i * width, high - width), width))
        return carry

    lax.fori_loop(0, -(-(high - low) // width), step, 0)


def width(steps):
    return max(1, 24 // steps)


def moved(at, by):
    return pl.ds(at.start + by, at.size)


def masks():
    lane = lax.broadcasted_iota(jnp.int32, (8, 128), 1)
    row = lax.broadcasted_iota(jnp.int32, (8, 128), 0)
    y = lane % SIDE
    return y != SIDE - 1, y != 0, lane < 96, lane >= 32, row < 7, row > 0


def beside(p, m):
    shape = p.shape
    p = p.reshape((-1,) + shape[-2:])
    y_up, y_down, x_in, x_out, row_up, row_down = [jnp.broadcast_to(a[None], p.shape) for a in m]
    zero = jnp.zeros_like(p)
    up = pltpu.roll(p, 96, 2)
    down = pltpu.roll(p, 32, 2)
    total = jnp.where(y_up, pltpu.roll(p, 127, 2), zero) + jnp.where(y_down, pltpu.roll(p, 1, 2), zero)
    total = total + jnp.where(x_in, up, jnp.where(row_up, pltpu.roll(up, 7, 1), zero))
    total = total + jnp.where(x_out, down, jnp.where(row_down, pltpu.roll(down, 1, 1), zero))
    return total.reshape(shape)


def spread(ref, t0, t1, z, m):
    p = ref[t0:t1, z]
    return p, beside(p, m) + ref[t0:t1, moved(z, -1)] + ref[t0:t1, moved(z, 1)]


def turn_in(ref, store):
    for s in range(8):
        store(s, ref[s * 128 : (s + 1) * 128, :].T)


def turn_out(ref, out):
    for s in range(8):
        out[s * 128 : (s + 1) * 128, :] = ref[:, s, :].T


def share_edges(odd, ref, edge_a, edge_b):
    n = edge_a.shape[1]
    far = OWN - n
    edge_a[...] = ref[:, pl.ds(far * (1 - odd), n)]
    edge_b[...] = ref[:, pl.ds(far * odd, n)]


def step_over(odd, src, row, edge_a, edge_b, edge_row, fn):
    m = masks()
    t = slice(row, row + 1)
    a = edge_a[edge_row : edge_row + 1]
    b = edge_b[edge_row : edge_row + 1]
    low = jnp.where(odd > 0, a, b)
    high = jnp.where(odd > 0, b, a)
    p = src[t, 0:1]
    fn(pl.ds(0, 1), p, beside(p, m) + low + src[t, 1:2])
    p = src[t, OWN - 1 : OWN]
    fn(pl.ds(OWN - 1, 1), p, beside(p, m) + high + src[t, OWN - 2 : OWN - 1])
    planes(1, OWN - 1, 18, lambda z: fn(z, *spread(src, row, row + 1, z, m)))


def swept(fixed, step, z, p, near, before):
    g = fixed[step : step + 1, z]
    return keep * p + fixed[3, z] * (g + base_coef * before[0:1, z] + fixed[2, z] * near)


def left(fixed, step, z, p, near, before):
    d = fixed[2, z]
    known = fixed[step : step + 1, z] + base_coef * before[0:1, z] + d * near
    return known - (base_coef + 6.0 * d) * p


def sweep_late(flag, fixed, x, x_a, x_b, y1, out_a, out_b):
    odd = flag[0]

    def fn(z, p, near):
        y1[:, z] = swept(fixed, 1, z, p, near, x)

    step_over(odd, x, 1, x_a, x_b, 1, fn)
    share_edges(odd, y1, out_a, out_b)


def sweep_both(flag, fixed, x, x_a, x_b, prev, y1, y1_a, y1_b, y0, z1, out_a, out_b):
    odd = flag[0]

    def early(z, p, near):
        y0[:, z] = swept(fixed, 0, z, p, near, prev)

    step_over(odd, x, 0, x_a, x_b, 0, early)

    def late(z, p, near):
        z1[:, z] = swept(fixed, 1, z, p, near, y0)

    step_over(odd, y1, 0, y1_a, y1_b, 0, late)
    share_edges(odd, y0, out_a.at[0:1], out_b.at[0:1])
    share_edges(odd, z1, out_a.at[1:2], out_b.at[1:2])


def sweep_both_raw(flag, fixed, x, x_a, x_b, back, y1, y1_a, y1_b, y0, z1, out_a, out_b, prev):
    def store(s, block):
        prev[0, :, s, :] = block

    turn_in(back.at[0], store)
    sweep_both(flag, fixed, x, x_a, x_b, prev, y1, y1_a, y1_b, y0, z1, out_a, out_b)


def sweep_early(flag, fixed, y0, y_a, y_b, prev, z0, out_a, out_b):
    odd = flag[0]

    def fn(z, p, near):
        z0[:, z] = swept(fixed, 0, z, p, near, prev)

    step_over(odd, y0, 0, y_a, y_b, 0, fn)
    share_edges(odd, z0, out_a, out_b)


def turned(flag, v_ref, g_ref, d_ref, v0, fixed, edge_a, edge_b):
    def into(ref, row):
        def store(s, block):
            ref[row, :, s, :] = block

        return store

    for t in range(2):
        turn_in(v_ref.at[t], into(v0, t))
    share_edges(flag[0], v0, edge_a, edge_b)
    for t in range(2):
        turn_in(g_ref.at[t], into(fixed, t))
    turn_in(d_ref, into(fixed, 2))

    def scale(z):
        fixed[3, z] = damping / (base_coef + 6.0 * fixed[2, z])

    planes(0, OWN, 8, scale)


def restrict_left(flag, fixed, z0, z1, e0a, e0b, e1a, e1b, prev, out, out_a, out_b):
    odd = flag[0]

    def early(z, p, near):
        out[0:1, z] = 0.5 * left(fixed, 0, z, p, near, prev)
        out[1:2, z] = fixed[2:3, z]

    def late(z, p, near):
        out[0:1, z] += 0.5 * left(fixed, 1, z, p, near, z0)

    step_over(odd, z0, 0, e0a, e0b, 0, early)
    step_over(odd, z1, 0, e1a, e1b, 1, late)
    share_edges(odd, out, out_a, out_b)


def cut(flag, own, edge_a, edge_b, pieces, d_piece, tall):
    odd = flag[0]
    end = OWN + HALO
    tall[:, pl.ds(end * (1 - odd), HALO)] = edge_a[...]
    tall[:, pl.ds(end * odd, HALO)] = edge_b[...]

    def copy(z):
        tall[:, moved(z, HALO)] = own[:, z]

    planes(0, OWN, 8, copy)
    for i in range(GROUP):
        pieces[i] = tall[0, i * PIECE : i * PIECE + WIDE]
    d_piece[...] = tall[1, pl.ds(flag[1], WIDE)]


def corrected_late(
    flag, fixed, z0, z1, e0a, e0b, e1a, e1b, e, e_a, e_b, x, x_a, x_b, y1, out_a, out_b
):
    def add(z):
        x[0:1, z] = z0[:, z] + e[:, z]
        x[1:2, z] = z1[:, z] + e[:, z]

    planes(0, OWN, 8, add)
    x_a[0:1] = e0a[...] + e_a[...]
    x_b[0:1] = e0b[...] + e_b[...]
    x_a[1:2] = e1a[1:2] + e_a[...]
    x_b[1:2] = e1b[1:2] + e_b[...]
    sweep_late(flag, fixed, x, x_a, x_b, y1, out_a, out_b)


def corrected_both(
    flag, fixed, x, x_a, x_b, prev, e_prev, y1, y1_a, y1_b, y0, z1, out_a, out_b, total
):
    def add(z):
        total[:, z] = prev[:, z] + e_prev[:, z]

    planes(0, OWN, 8, add)
    sweep_both(flag, fixed, x, x_a, x_b, total, y1, y1_a, y1_b, y0, z1, out_a, out_b)


def finish(flag, fixed, z0, z1, e0a, e0b, e1a, e1b, prev, sol_out, res_out, res):
    odd = flag[0]
    turn_out(z0.at[0], sol_out.at[0])
    turn_out(z1.at[0], sol_out.at[1])

    def late(z, p, near):
        res[1:2, z] = left(fixed, 1, z, p, near, z0)

    def early(z, p, near):
        res[0:1, z] = left(fixed, 0, z, p, near, prev)

    step_over(odd, z1, 0, e1a, e1b, 1, late)
    turn_out(res.at[1], res_out.at[1])
    step_over(odd, z0, 0, e0a, e0b, 0, early)
    turn_out(res.at[0], res_out.at[0])


def step_down(flag, d_ref, *refs, counts, own, c, low, last, tail_steps):
    history = refs[: len(counts)]
    g_own = refs[len(counts)]
    rest = refs[len(counts) + 1 :]
    past = sum(counts)
    total = past + own
    high = WIDE - low
    q = flag[0]
    if last:
        v_above, e_ref, tail, s_ref, g_ref, va, vb = rest
    elif tail_steps:
        v2, below, tail, s_ref, g_ref, va = rest
    else:
        v2, below, s_ref, g_ref, va = rest

    def gather(z):
        s = damping / (c + 6.0 * d_ref[z])
        s_ref[z] = s
        at = 0
        for i, (ref, n) in enumerate(zip(history, counts)):
            known = jnp.where(q > len(counts) - 1 - i, 1.0, 0.0).astype(F32)
            g = known * ref[:, moved(z, -low)]
            g_ref[at : at + n, z] = g
            va[at : at + n, z] = s * g
            at += n
        g = g_own[:, moved(z, -low)]
        g_ref[at:, z] = g
        va[at:, z] = s * g

    planes(low, high, width(total), gather)
    m = masks()

    def sweep(src, start, margin, store):
        def fn(z):
            p, near = spread(src, start, total, z, m)
            value = keep * p + s_ref[z] * (
                g_ref[start:total, z] + c * src[start - 1 : total - 1, z] + d_ref[z] * near
            )
            store(z, value)

        planes(low + margin, high - margin, width(total - start), fn)

    if last:

        def keep_b(z, value):
            vb[1:total, z] = value

        def keep_a(z, value):
            va[2:total, z] = value

        def keep_e(z, value):
            e_ref[:, moved(z, -low - 3)] = value
            tail[:, moved(z, -low - 3)] = v_above[v_above.shape[0] - 2 :, moved(z, 1 - low)] + value

        sweep(va, 1, 1, keep_b)
        sweep(vb, 2, 2, keep_a)
        sweep(va, 3, 3, keep_e)
        return

    def keep_v(z, value):
        v2[:, moved(z, -low - 1)] = value

    sweep(va, 1, 1, keep_v)

    def left(z):
        zz = moved(z, -low - 1)
        p, near = spread(v2, past - 1, total - 1, zz, m)
        d = d_ref[z]
        r = g_ref[past:total, z] + c * v2[past - 2 : total - 2, zz] + d * near - (c + 6.0 * d) * p
        for j in range(own // 2):
            value = 0.5 * (r[2 * j] + r[2 * j + 1])
            below[j, moved(z, -low - 2)] = value
            if tail_steps and j >= own // 2 - tail_steps:
                tail[j - own // 2 + tail_steps, moved(z, -low - 2)] = value

    planes(low + 2, high - 2, width(own), left)


def step_up(flag, d_ref, v2, g_last, g_own, v_last, e_own, *rest, own, c, low, e_low, top):
    if top:
        out, s_ref, va, vb = rest
    else:
        v_above, out, tail, s_ref, va, vb = rest
    q = flag[0]
    known = jnp.where(q > 0, 1.0, 0.0).astype(F32)
    n = own + 2
    last = g_last.shape[0] - 1

    def correct(z):
        s_ref[z] = damping / (c + 6.0 * d_ref[z])
        zz = moved(z, -low - 1)
        here = moved(z, -e_low)
        va[0:2, z] = known * v_last[:, here]
        for j in range(own // 2):
            e = e_own[j, here]
            va[2 + 2 * j, z] = v2[1 + 2 * j, zz] + e
            va[3 + 2 * j, z] = v2[2 + 2 * j, zz] + e

    planes(e_low, WIDE - e_low, width(n), correct)
    m = masks()

    def sweep1(z):
        p, near = spread(va, 1, n, z, m)
        g0 = known * g_last[last : last + 1, moved(z, -low)]
        g = jnp.concatenate([g0, g_own[:, moved(z, -low)]], axis=0)
        vb[:, z] = keep * p + s_ref[z] * (g + c * va[0 : n - 1, z] + d_ref[z] * near)

    planes(e_low + 1, WIDE - e_low - 1, width(n - 1), sweep1)

    def sweep2(z):
        p, near = spread(vb, 1, n - 1, z, m)
        value = keep * p + s_ref[z] * (
            g_own[:, moved(z, -low)] + c * vb[0 : n - 2, z] + d_ref[z] * near
        )
        here = moved(z, -e_low - 2)
        out[:, here] = value
        if not top:
            tail[:, here] = v_above[v_above.shape[0] - 2 :, moved(z, 1 - low)] + value[own - 1 :]

    planes(e_low + 2, WIDE - e_low - 2, width(own), sweep2)


def later(block, distance):
    count = lax.axis_size("tm")
    return lax.ppermute(block, "tm", [(i, i + distance) for i in range(count - distance)])


def around(block, distance):
    count = lax.axis_size("tm")
    return lax.ppermute(block, "tm", [(i, (i + distance) % count) for i in range(count)])


def body(source, initial_guess, diffusivity):
    T = (8, 128)
    slabs = lax.axis_size("gz")
    count = lax.axis_size("tm")
    odd = (lax.axis_index("gz") % 2).astype(jnp.int32).reshape(1)
    me = lax.axis_index("tm").astype(jnp.int32)
    q = (me // GROUP).reshape(1)
    piece = jnp.concatenate([odd, (me % GROUP * PIECE).reshape(1)])
    pairs = [(i, i + 1) for i in range(1, slabs - 1, 2)]
    pairs = pairs + [(b, a) for a, b in pairs]

    def swapped(edge_a, edge_b):
        return (
            lax.ppermute(edge_a, "gz", [(i, i ^ 1) for i in range(slabs)]),
            lax.ppermute(edge_b, "gz", pairs),
        )

    flat = lambda a: a.reshape(a.shape[:-3] + (SIDE * SIDE, OWN))
    guess = flat(initial_guess)
    prev = later(guess[1:2], 1)
    plane = (1, OWN) + T
    edge = [(1, 1) + T] * 2
    edges = [(2, 1) + T] * 2
    run = functools.partial(call, n_scalar=1)
    x, fixed, *ends = run(
        turned,
        [(2, OWN) + T, (4, OWN) + T] + edges,
        (odd, guess, flat(source), flat(diffusivity)),
    )
    x = (x, *swapped(*ends))
    y1, *ends = run(sweep_late, [plane] + edge, (odd, fixed, *x))
    y1_prev = later(y1, 1)
    y0, z1, *ends = run(
        sweep_both_raw,
        [plane, plane] + edges,
        (odd, fixed, *x, prev, y1, *swapped(*ends)),
        scratch=[plane],
    )
    v2_prev = later(z1, 1)
    late_ends = swapped(*ends)
    z0, *ends = run(sweep_early, [plane] + edge, (odd, fixed, y0, *late_ends, y1_prev))
    v2 = (z0, z1, *swapped(*ends), *late_ends)
    g1, *ends = run(
        restrict_left, [(2, OWN) + T] + [(2, HALO) + T] * 2, (odd, fixed, *v2, v2_prev)
    )
    pieces, d = call(
        cut,
        [(GROUP, WIDE) + T, (WIDE,) + T],
        (piece, g1, *swapped(*ends)),
        scratch=[(2, OWN + 2 * HALO) + T],
        n_scalar=1,
    )
    groups = [list(range(a, a + GROUP)) for a in range(0, count, GROUP)]
    g = lax.all_to_all(pieces, "tm", 0, 0, axis_index_groups=groups, tiled=True)

    saved = []
    own_steps = GROUP
    c = base_coef / 2.0
    low = 0
    g_tail = g[-2:]
    for level in range(1, 4):
        history = around(g_tail, GROUP)
        total = own_steps + 2
        wide = WIDE - 2 * low
        tail_steps = 2 if own_steps > 4 else 0
        v, g_below, *g_tail = call(
            functools.partial(
                step_down, counts=[2], own=own_steps, c=c, low=low, last=False, tail_steps=tail_steps
            ),
            [(total - 1, wide - 2) + T, (own_steps // 2, wide - 4) + T]
            + [(tail_steps, wide - 4) + T] * (tail_steps > 0),
            (q, d, history, g),
            scratch=[(WIDE,) + T, (total, WIDE) + T, (total, WIDE) + T],
            n_scalar=1,
        )
        g_tail = g_tail[0] if g_tail else g_below
        saved.append((v, history, g, own_steps, c, low))
        g = g_below
        own_steps //= 2
        c /= 2.0
        low += 2
    history = [around(g, i * GROUP) for i in (3, 2, 1)]
    wide = WIDE - 2 * low
    e, tail = call(
        functools.partial(
            step_down, counts=[1] * 3, own=1, c=c, low=low, last=True, tail_steps=0
        ),
        [(1, wide - 6) + T, (2, wide - 6) + T],
        (q, d, *history, g, saved[-1][0]),
        scratch=[(WIDE,) + T] + [(4, WIDE) + T] * 3,
        n_scalar=1,
    )
    e_low = low + 3
    while saved:
        v, g_last, g, own_steps, c, low = saved.pop()
        v_last = around(tail, GROUP)
        top = not saved
        narrow = WIDE - 2 * e_low - 4
        e = call(
            functools.partial(step_up, own=own_steps, c=c, low=low, e_low=e_low, top=top),
            [(own_steps, narrow) + T] + [(2, narrow) + T] * (not top),
            (q, d, v, g_last, g, v_last, e) + (() if top else (saved[-1][0],)),
            scratch=[(WIDE,) + T, (own_steps + 2, WIDE) + T, (own_steps + 1, WIDE) + T],
            n_scalar=1,
        )
        tail = e[-1]
        e = e[0]
        e_low += 2
    e0 = lax.all_to_all(e, "tm", 0, 0, axis_index_groups=groups, tiled=True)
    e0 = e0.reshape((1, OWN) + T)
    e_prev = later(e0, 1)
    side = (OWN - 1) * (1 - odd[0])
    e_a = lax.dynamic_slice_in_dim(e0, side, 1, axis=1)
    e_b = lax.dynamic_slice_in_dim(e0, OWN - 1 - side, 1, axis=1)
    *x, y1, out_a, out_b = run(
        corrected_late,
        [(2, OWN) + T] + edges + [plane] + edge,
        (odd, fixed, *v2, e0, *swapped(e_a, e_b)),
    )
    y1_prev = later(y1, 1)
    y0, z1, *ends = run(
        corrected_both,
        [plane, plane] + edges,
        (odd, fixed, *x, v2_prev, e_prev, y1, *swapped(out_a, out_b)),
        scratch=[plane],
    )
    prev = later(z1, 1)
    late_ends = swapped(*ends)
    z0, *ends = run(sweep_early, [plane] + edge, (odd, fixed, y0, *late_ends, y1_prev))
    sol, res = run(
        finish,
        [(2, SIDE * SIDE, OWN)] * 2,
        (odd, fixed, z0, z1, *swapped(*ends), *late_ends, prev),
        scratch=[(2, OWN) + T],
    )
    return sol.reshape(source.shape), res.reshape(source.shape)


def solution(mesh):
    placed = (P("tm", None, None, "gz"), P("tm", None, None, "gz"), P(None, None, "gz"))
    return jax.shard_map(
        body,
        mesh=mesh,
        in_specs=placed,
        out_specs=(P("tm", None, None, "gz"), P("tm", None, None, "gz")),
        check_vma=False,
    )
```

```python
import functools
import math
import jax
import jax.numpy as jnp
from jax import lax
from jax.experimental import pallas as pl
from jax.experimental.pallas import tpu as pltpu
from jax.sharding import PartitionSpec as P

damping = 0.8
keep = 1.0 - 0.8
base_coef = 8.0

SIDE = 32
OWN = 128
GROUP = 8
PIECE = OWN // GROUP
HALO = 15
WIDE = PIECE + 2 * HALO
F32 = jnp.float32

VM = pl.BlockSpec(memory_space=pltpu.VMEM)
SM = pl.BlockSpec(memory_space=pltpu.SMEM)


def call(body, outs, args, scratch=(), n_scalar=0):
    single = isinstance(outs, tuple)
    shapes = [outs] if single else list(outs)
    held = shapes + list(scratch) + [a.shape for a in args[n_scalar:]]
    need = sum(4 * math.prod(s) for s in held)
    result = pl.pallas_call(
        body,
        out_shape=[jax.ShapeDtypeStruct(s, F32) for s in shapes],
        in_specs=[SM] * n_scalar + [VM] * (len(args) - n_scalar),
        out_specs=[VM] * len(shapes),
        scratch_shapes=[pltpu.VMEM(s, F32) for s in scratch],
        compiler_params=pltpu.CompilerParams(vmem_limit_bytes=need + (2 << 20)),
    )(*args)
    return result[0] if single else result


def planes(low, high, width, fn):
    width = min(width, high - low)

    def step(i, carry):
        fn(pl.ds(jnp.minimum(low + i * width, high - width), width))
        return carry

    lax.fori_loop(0, -(-(high - low) // width), step, 0)


def width(steps):
    return max(1, 24 // steps)


def moved(at, by):
    return pl.ds(at.start + by, at.size)


def masks():
    lane = lax.broadcasted_iota(jnp.int32, (8, 128), 1)
    row = lax.broadcasted_iota(jnp.int32, (8, 128), 0)
    y = lane % SIDE
    return y != SIDE - 1, y != 0, lane < 96, lane >= 32, row < 7, row > 0


def beside(p, m):
    shape = p.shape
    p = p.reshape((-1,) + shape[-2:])
    y_up, y_down, x_in, x_out, row_up, row_down = [jnp.broadcast_to(a[None], p.shape) for a in m]
    zero = jnp.zeros_like(p)
    up = pltpu.roll(p, 96, 2)
    down = pltpu.roll(p, 32, 2)
    total = jnp.where(y_up, pltpu.roll(p, 127, 2), zero) + jnp.where(y_down, pltpu.roll(p, 1, 2), zero)
    total = total + jnp.where(x_in, up, jnp.where(row_up, pltpu.roll(up, 7, 1), zero))
    total = total + jnp.where(x_out, down, jnp.where(row_down, pltpu.roll(down, 1, 1), zero))
    return total.reshape(shape)


def spread(ref, t0, t1, z, m):
    p = ref[t0:t1, z]
    return p, beside(p, m) + ref[t0:t1, moved(z, -1)] + ref[t0:t1, moved(z, 1)]


def turn_in(ref, store):
    for s in range(8):
        store(s, ref[s * 128 : (s + 1) * 128, :].T)


def turn_out(ref, out):
    for s in range(8):
        out[s * 128 : (s + 1) * 128, :] = ref[:, s, :].T


def share_edges(odd, ref, edge_a, edge_b):
    n = edge_a.shape[1]
    far = OWN - n
    edge_a[...] = ref[:, pl.ds(far * (1 - odd), n)]
    edge_b[...] = ref[:, pl.ds(far * odd, n)]


def step_over(odd, src, row, edge_a, edge_b, edge_row, fn):
    m = masks()
    t = slice(row, row + 1)
    a = edge_a[edge_row : edge_row + 1]
    b = edge_b[edge_row : edge_row + 1]
    low = jnp.where(odd > 0, a, b)
    high = jnp.where(odd > 0, b, a)
    p = src[t, 0:1]
    fn(pl.ds(0, 1), p, beside(p, m) + low + src[t, 1:2])
    p = src[t, OWN - 1 : OWN]
    fn(pl.ds(OWN - 1, 1), p, beside(p, m) + high + src[t, OWN - 2 : OWN - 1])
    planes(1, OWN - 1, 18, lambda z: fn(z, *spread(src, row, row + 1, z, m)))


def swept(fixed, step, z, p, near, before):
    g = fixed[step : step + 1, z]
    return keep * p + fixed[3, z] * (g + base_coef * before[0:1, z] + fixed[2, z] * near)


def left(fixed, step, z, p, near, before):
    d = fixed[2, z]
    known = fixed[step : step + 1, z] + base_coef * before[0:1, z] + d * near
    return known - (base_coef + 6.0 * d) * p


def sweep_late(flag, fixed, x, x_a, x_b, y1, out_a, out_b):
    odd = flag[0]

    def fn(z, p, near):
        y1[:, z] = swept(fixed, 1, z, p, near, x)

    step_over(odd, x, 1, x_a, x_b, 1, fn)
    share_edges(odd, y1, out_a, out_b)


def sweep_both(flag, fixed, x, x_a, x_b, prev, y1, y1_a, y1_b, y0, z1, out_a, out_b):
    odd = flag[0]

    def early(z, p, near):
        y0[:, z] = swept(fixed, 0, z, p, near, prev)

    step_over(odd, x, 0, x_a, x_b, 0, early)

    def late(z, p, near):
        z1[:, z] = swept(fixed, 1, z, p, near, y0)

    step_over(odd, y1, 0, y1_a, y1_b, 0, late)
    share_edges(odd, y0, out_a.at[0:1], out_b.at[0:1])
    share_edges(odd, z1, out_a.at[1:2], out_b.at[1:2])


def sweep_both_raw(flag, fixed, x, x_a, x_b, back, y1, y1_a, y1_b, y0, z1, out_a, out_b, prev):
    def store(s, block):
        prev[0, :, s, :] = block

    turn_in(back.at[0], store)
    sweep_both(flag, fixed, x, x_a, x_b, prev, y1, y1_a, y1_b, y0, z1, out_a, out_b)


def sweep_early(flag, fixed, y0, y_a, y_b, prev, z0, out_a, out_b):
    odd = flag[0]

    def fn(z, p, near):
        z0[:, z] = swept(fixed, 0, z, p, near, prev)

    step_over(odd, y0, 0, y_a, y_b, 0, fn)
    share_edges(odd, z0, out_a, out_b)


def turned(flag, v_ref, g_ref, d_ref, v0, fixed, edge_a, edge_b):
    def into(ref, row):
        def store(s, block):
            ref[row, :, s, :] = block

        return store

    for t in range(2):
        turn_in(v_ref.at[t], into(v0, t))
    share_edges(flag[0], v0, edge_a, edge_b)
    for t in range(2):
        turn_in(g_ref.at[t], into(fixed, t))
    turn_in(d_ref, into(fixed, 2))

    def scale(z):
        fixed[3, z] = damping / (base_coef + 6.0 * fixed[2, z])

    planes(0, OWN, 8, scale)


def restrict_left(flag, fixed, z0, z1, e0a, e0b, e1a, e1b, prev, out, out_a, out_b):
    odd = flag[0]

    def early(z, p, near):
        out[:, z] += 0.5 * left(fixed, 0, z, p, near, prev)

    def late(z, p, near):
        out[:, z] = 0.5 * left(fixed, 1, z, p, near, z0)

    step_over(odd, z1, 0, e1a, e1b, 1, late)
    step_over(odd, z0, 0, e0a, e0b, 0, early)
    share_edges(odd, out, out_a.at[0:1], out_b.at[0:1])
    share_edges(odd, fixed.at[2:3], out_a.at[1:2], out_b.at[1:2])


def cut(flag, own, fixed, edge_a, edge_b, pieces, d_piece, tall):
    odd = flag[0]
    end = OWN + HALO
    tall[:, pl.ds(end * (1 - odd), HALO)] = edge_a[...]
    tall[:, pl.ds(end * odd, HALO)] = edge_b[...]

    def copy(z):
        tall[0:1, moved(z, HALO)] = own[:, z]
        tall[1:2, moved(z, HALO)] = fixed[2:3, z]

    planes(0, OWN, 8, copy)
    for i in range(GROUP):
        pieces[i] = tall[0, i * PIECE : i * PIECE + WIDE]
    d_piece[...] = tall[1, pl.ds(flag[1], WIDE)]


def corrected_late(
    flag, fixed, z0, z1, e0a, e0b, e1a, e1b, e, e_a, e_b, x, x_a, x_b, y1, out_a, out_b
):
    def add(z):
        x[0:1, z] = z0[:, z] + e[:, z]
        x[1:2, z] = z1[:, z] + e[:, z]

    planes(0, OWN, 8, add)
    x_a[0:1] = e0a[...] + e_a[...]
    x_b[0:1] = e0b[...] + e_b[...]
    x_a[1:2] = e1a[1:2] + e_a[...]
    x_b[1:2] = e1b[1:2] + e_b[...]
    sweep_late(flag, fixed, x, x_a, x_b, y1, out_a, out_b)


def corrected_both(
    flag, fixed, x, x_a, x_b, prev, e_prev, y1, y1_a, y1_b, y0, z1, out_a, out_b, total
):
    def add(z):
        total[:, z] = prev[:, z] + e_prev[:, z]

    planes(0, OWN, 8, add)
    sweep_both(flag, fixed, x, x_a, x_b, total, y1, y1_a, y1_b, y0, z1, out_a, out_b)


def finish_late(flag, fixed, z0, z1, e1a, e1b, sol_out, res):
    turn_out(z0.at[0], sol_out.at[0])
    turn_out(z1.at[0], sol_out.at[1])

    def late(z, p, near):
        res[:, z] = left(fixed, 1, z, p, near, z0)

    step_over(flag[0], z1, 0, e1a, e1b, 1, late)


def finish_early(flag, fixed, z0, e0a, e0b, prev, late, res_out, res):
    turn_out(late.at[0], res_out.at[1])

    def early(z, p, near):
        res[:, z] = left(fixed, 0, z, p, near, prev)

    step_over(flag[0], z0, 0, e0a, e0b, 0, early)
    turn_out(res.at[0], res_out.at[0])


def step_alone(d_ref, g_own, v2, below, tail, s_ref, va, *, c):
    n = g_own.shape[0]
    m = masks()

    def gather(z):
        s = damping / (c + 6.0 * d_ref[z])
        s_ref[z] = s
        va[:, z] = s * g_own[:, z]

    planes(0, WIDE, width(n), gather)

    def sweep(z):
        p, near = spread(va, 1, n, z, m)
        v2[:, moved(z, -1)] = keep * p + s_ref[z] * (
            g_own[1:n, z] + c * va[0 : n - 1, z] + d_ref[z] * near
        )

    planes(1, WIDE - 1, width(n - 1), sweep)

    def left(z):
        zz = moved(z, -1)
        p, near = spread(v2, 1, n - 1, zz, m)
        d = d_ref[z]
        r = g_own[2:n, z] + c * v2[0 : n - 2, zz] + d * near - (c + 6.0 * d) * p
        for j in range(n // 2 - 1):
            value = 0.5 * (r[2 * j] + r[2 * j + 1])
            below[j, moved(z, -2)] = value
            if j >= n // 2 - 3:
                tail[j - n // 2 + 3, moved(z, -2)] = value

    planes(2, WIDE - 2, width(n - 2), left)


def step_join(flag, d_ref, history, g_own, v2, first, below, kept, s_ref, g_ref, va, vb, *, c, keep_low):
    known = jnp.where(flag[0] > 0, 1.0, 0.0).astype(F32)
    m = masks()

    def gather(z):
        s = damping / (c + 6.0 * d_ref[z])
        s_ref[z] = s
        g = known * history[:, z]
        g_ref[0:2, z] = g
        va[0:2, z] = s * g
        g = g_own[0:1, z]
        g_ref[2:3, z] = g
        va[2:3, z] = s * g

    planes(0, WIDE, 8, gather)

    def sweep(z):
        p, near = spread(va, 1, 3, z, m)
        value = keep * p + s_ref[z] * (g_ref[1:3, z] + c * va[0:2, z] + d_ref[z] * near)
        vb[0:2, z] = value
        vb[2, z] = v2[0, moved(z, -1)]
        first[:, moved(z, -1)] = value[1:2]

    planes(1, WIDE - 1, 10, sweep)

    def left(z):
        p, near = spread(vb, 1, 3, z, m)
        d = d_ref[z]
        r = g_own[0:2, z] + c * vb[0:2, z] + d * near - (c + 6.0 * d) * p
        below[0, moved(z, -2)] = 0.5 * (r[0] + r[1])

    planes(2, WIDE - 2, 10, left)
    kept[0:1] = g_ref[1:2, keep_low : WIDE - keep_low]
    kept[1:] = g_own[:, keep_low : WIDE - keep_low]


def step_down(flag, d_ref, *refs, parts, c, low, last, keep_low):
    arrays = refs[: len(parts)]
    rest = refs[len(parts) :]
    past = sum(n for n, need in parts if need)
    total = sum(n for n, need in parts)
    own = total - past
    high = WIDE - low
    q = flag[0]
    if last:
        v_above, e_ref, tail, s_ref, g_ref, va, vb = rest
    else:
        v2, below, kept, s_ref, g_ref, va = rest

    def gather(z):
        s = damping / (c + 6.0 * d_ref[z])
        s_ref[z] = s
        at = 0
        for ref, (n, need) in zip(arrays, parts):
            g = ref[:, moved(z, -low)]
            if need:
                g = jnp.where(q >= need, 1.0, 0.0).astype(F32) * g
            g_ref[at : at + n, z] = g
            va[at : at + n, z] = s * g
            at += n

    planes(low, high, width(total), gather)
    m = masks()

    def sweep(src, start, margin, store):
        def fn(z):
            p, near = spread(src, start, total, z, m)
            value = keep * p + s_ref[z] * (
                g_ref[start:total, z] + c * src[start - 1 : total - 1, z] + d_ref[z] * near
            )
            store(z, value)

        planes(low + margin, high - margin, width(total - start), fn)

    if last:

        def keep_b(z, value):
            vb[1:total, z] = value

        def keep_a(z, value):
            va[2:total, z] = value

        def keep_e(z, value):
            e_ref[:, moved(z, -low - 3)] = value
            tail[:, moved(z, -low - 3)] = v_above[v_above.shape[0] - 2 :, moved(z, 1 - low)] + value

        sweep(va, 1, 1, keep_b)
        sweep(vb, 2, 2, keep_a)
        sweep(va, 3, 3, keep_e)
        return

    def keep_v(z, value):
        v2[:, moved(z, -low - 1)] = value

    sweep(va, 1, 1, keep_v)

    def left(z):
        zz = moved(z, -low - 1)
        p, near = spread(v2, past - 1, total - 1, zz, m)
        d = d_ref[z]
        r = g_ref[past:total, z] + c * v2[past - 2 : total - 2, zz] + d * near - (c + 6.0 * d) * p
        for j in range(own // 2):
            below[j, moved(z, -low - 2)] = 0.5 * (r[2 * j] + r[2 * j + 1])

    planes(low + 2, high - 2, width(own), left)
    kept[...] = g_ref[past - 1 :, keep_low : WIDE - keep_low]


def step_up(flag, d_ref, kept, v_last, e_own, *refs, firsts, own, c, low, e_low, top):
    values = refs[: len(firsts)]
    if top:
        out, s_ref, va, vb = refs[len(firsts) :]
    else:
        v_above, out, tail, s_ref, va, vb = refs[len(firsts) :]
    known = jnp.where(flag[0] > 0, 1.0, 0.0).astype(F32)
    n = own + 2

    def correct(z):
        s_ref[z] = damping / (c + 6.0 * d_ref[z])
        zz = moved(z, -low - 1)
        here = moved(z, -e_low)
        va[0:2, z] = known * v_last[:, here]
        for step in range(own):
            ref, first = [(r, f) for r, f in zip(values, firsts) if f <= step][-1]
            va[2 + step, z] = ref[step - first, zz] + e_own[step // 2, here]

    planes(e_low, WIDE - e_low, width(n), correct)
    m = masks()

    def sweep1(z):
        p, near = spread(va, 1, n, z, m)
        g = kept[:, moved(z, -e_low - 1)]
        vb[:, z] = keep * p + s_ref[z] * (g + c * va[0 : n - 1, z] + d_ref[z] * near)

    planes(e_low + 1, WIDE - e_low - 1, width(n - 1), sweep1)

    def sweep2(z):
        p, near = spread(vb, 1, n - 1, z, m)
        g = kept[1:, moved(z, -e_low - 1)]
        value = keep * p + s_ref[z] * (g + c * vb[0 : n - 2, z] + d_ref[z] * near)
        here = moved(z, -e_low - 2)
        out[:, here] = value
        if not top:
            tail[:, here] = v_above[v_above.shape[0] - 2 :, moved(z, 1 - low)] + value[own - 1 :]

    planes(e_low + 2, WIDE - e_low - 2, width(own), sweep2)


def later(block, distance):
    count = lax.axis_size("tm")
    return lax.ppermute(block, "tm", [(i, i + distance) for i in range(count - distance)])


def around(block, distance):
    count = lax.axis_size("tm")
    return lax.ppermute(block, "tm", [(i, (i + distance) % count) for i in range(count)])


def body(source, initial_guess, diffusivity):
    T = (8, 128)
    slabs = lax.axis_size("gz")
    count = lax.axis_size("tm")
    odd = (lax.axis_index("gz") % 2).astype(jnp.int32).reshape(1)
    me = lax.axis_index("tm").astype(jnp.int32)
    q = (me // GROUP).reshape(1)
    piece = jnp.concatenate([odd, (me % GROUP * PIECE).reshape(1)])
    pairs = [(i, i + 1) for i in range(1, slabs - 1, 2)]
    pairs = pairs + [(b, a) for a, b in pairs]

    def swapped(edge_a, edge_b):
        return (
            lax.ppermute(edge_a, "gz", [(i, i ^ 1) for i in range(slabs)]),
            lax.ppermute(edge_b, "gz", pairs),
        )

    flat = lambda a: a.reshape(a.shape[:-3] + (SIDE * SIDE, OWN))
    guess = flat(initial_guess)
    prev = later(guess[1:2], 1)
    plane = (1, OWN) + T
    edge = [(1, 1) + T] * 2
    edges = [(2, 1) + T] * 2
    run = functools.partial(call, n_scalar=1)
    x, fixed, *ends = run(
        turned,
        [(2, OWN) + T, (4, OWN) + T] + edges,
        (odd, guess, flat(source), flat(diffusivity)),
    )
    x = (x, *swapped(*ends))
    y1, *ends = run(sweep_late, [plane] + edge, (odd, fixed, *x))
    y1_prev = later(y1, 1)
    y0, z1, *ends = run(
        sweep_both_raw,
        [plane, plane] + edges,
        (odd, fixed, *x, prev, y1, *swapped(*ends)),
        scratch=[plane],
    )
    v2_prev = later(z1, 1)
    late_ends = swapped(*ends)
    z0, *ends = run(sweep_early, [plane] + edge, (odd, fixed, y0, *late_ends, y1_prev))
    v2 = (z0, z1, *swapped(*ends), *late_ends)
    g1, *ends = run(
        restrict_left, [plane] + [(2, HALO) + T] * 2, (odd, fixed, *v2, v2_prev)
    )
    pieces, d = call(
        cut,
        [(GROUP, WIDE) + T, (WIDE,) + T],
        (piece, g1, fixed, *swapped(*ends)),
        scratch=[(2, OWN + 2 * HALO) + T],
        n_scalar=1,
    )
    groups = [list(range(a, a + GROUP)) for a in range(0, count, GROUP)]
    g = lax.all_to_all(pieces, "tm", 0, 0, axis_index_groups=groups, tiled=True)

    c = base_coef / 2.0
    history = around(g[-2:], GROUP)
    n = GROUP
    v, g_rest, g_tail = call(
        functools.partial(step_alone, c=c),
        [(n - 1, WIDE - 2) + T, (n // 2 - 1, WIDE - 4) + T, (2, WIDE - 4) + T],
        (d, g),
        scratch=[(WIDE,) + T, (n, WIDE) + T],
    )
    next_history = around(g_tail, GROUP)
    first, g_first, kept = run(
        functools.partial(step_join, c=c, keep_low=14),
        [(1, WIDE - 2) + T, (1, WIDE - 4) + T, (n + 1, WIDE - 28) + T],
        (q, d, history, g, v),
        scratch=[(WIDE,) + T] + [(3, WIDE) + T] * 3,
    )
    saved = [((first, v), (0, 1), kept, n, c, 0)]
    parts = [(2, 1), (1, 0), (3, 0)]
    arrays = [next_history, g_first, g_rest]
    for level in (2, 3):
        n, c, low = n // 2, c / 2.0, 2 * level - 2
        wide = WIDE - 2 * low
        keep_low = 16 - 2 * level
        v, g, kept = run(
            functools.partial(
                step_down, parts=parts, c=c, low=low, last=False, keep_low=keep_low
            ),
            [(n + 1, wide - 2) + T, (n // 2, wide - 4) + T, (n + 1, WIDE - 2 * keep_low) + T],
            (q, d, *arrays),
            scratch=[(WIDE,) + T, (n + 2, WIDE) + T, (n + 2, WIDE) + T],
        )
        saved.append(((v,), (-1,), kept, n, c, low))
        if level == 2:
            parts = [(2, 1), (2, 0)]
            arrays = [around(g, GROUP), g]
    parts = [(1, 3), (1, 2), (1, 1), (1, 0)]
    arrays = [around(g, i * GROUP) for i in (3, 2, 1)] + [g]
    low = 6
    wide = WIDE - 2 * low
    e, tail = run(
        functools.partial(step_down, parts=parts, c=c / 2.0, low=low, last=True, keep_low=0),
        [(1, wide - 6) + T, (2, wide - 6) + T],
        (q, d, *arrays, saved[-1][0][-1]),
        scratch=[(WIDE,) + T] + [(4, WIDE) + T] * 3,
    )
    e_low = low + 3
    while saved:
        values, firsts, kept, n, c, low = saved.pop()
        v_last = around(tail, GROUP)
        top = not saved
        narrow = WIDE - 2 * e_low - 4
        e, *tail = run(
            functools.partial(
                step_up, firsts=firsts, own=n, c=c, low=low, e_low=e_low, top=top
            ),
            [(n, narrow) + T] + [(2, narrow) + T] * (not top),
            (q, d, kept, v_last, e, *values) + (() if top else (saved[-1][0][-1],)),
            scratch=[(WIDE,) + T, (n + 2, WIDE) + T, (n + 1, WIDE) + T],
        )
        tail = tail[0] if tail else None
        e_low += 2
    e0 = lax.all_to_all(e, "tm", 0, 0, axis_index_groups=groups, tiled=True)
    e0 = e0.reshape((1, OWN) + T)
    e_prev = later(e0, 1)
    side = (OWN - 1) * (1 - odd[0])
    e_a = lax.dynamic_slice_in_dim(e0, side, 1, axis=1)
    e_b = lax.dynamic_slice_in_dim(e0, OWN - 1 - side, 1, axis=1)
    *x, y1, out_a, out_b = run(
        corrected_late,
        [(2, OWN) + T] + edges + [plane] + edge,
        (odd, fixed, *v2, e0, *swapped(e_a, e_b)),
    )
    y1_prev = later(y1, 1)
    y0, z1, *ends = run(
        corrected_both,
        [plane, plane] + edges,
        (odd, fixed, *x, v2_prev, e_prev, y1, *swapped(out_a, out_b)),
        scratch=[plane],
    )
    prev = later(z1, 1)
    late_ends = swapped(*ends)
    z0, *ends = run(sweep_early, [plane] + edge, (odd, fixed, y0, *late_ends, y1_prev))
    sol, res = run(
        finish_late, [(2, SIDE * SIDE, OWN), plane], (odd, fixed, z0, z1, *late_ends)
    )
    res = run(
        finish_early,
        (2, SIDE * SIDE, OWN),
        (odd, fixed, z0, *swapped(*ends), prev, res),
        scratch=[plane],
    )
    return sol.reshape(source.shape), res.reshape(source.shape)


def solution(mesh):
    placed = (P("tm", None, None, "gz"), P("tm", None, None, "gz"), P(None, None, "gz"))
    return jax.shard_map(
        body,
        mesh=mesh,
        in_specs=placed,
        out_specs=(P("tm", None, None, "gz"), P("tm", None, None, "gz")),
        check_vma=False,
    )
```

```python
import functools
import math
import jax
import jax.numpy as jnp
from jax import lax
from jax.experimental import pallas as pl
from jax.experimental.pallas import tpu as pltpu
from jax.sharding import PartitionSpec as P

damping = 0.8
keep = 1.0 - 0.8
base_coef = 8.0

SIDE = 32
OWN = 128
GROUP = 8
PIECE = OWN // GROUP
HALO = 15
WIDE = PIECE + 2 * HALO
F32 = jnp.float32

VM = pl.BlockSpec(memory_space=pltpu.VMEM)
SM = pl.BlockSpec(memory_space=pltpu.SMEM)


def call(body, outs, args, scratch=(), n_scalar=0):
    single = isinstance(outs, tuple)
    shapes = [outs] if single else list(outs)
    held = shapes + list(scratch) + [a.shape for a in args[n_scalar:]]
    need = sum(4 * math.prod(s) for s in held)
    result = pl.pallas_call(
        body,
        out_shape=[jax.ShapeDtypeStruct(s, F32) for s in shapes],
        in_specs=[SM] * n_scalar + [VM] * (len(args) - n_scalar),
        out_specs=[VM] * len(shapes),
        scratch_shapes=[pltpu.VMEM(s, F32) for s in scratch],
        compiler_params=pltpu.CompilerParams(vmem_limit_bytes=need + (2 << 20)),
    )(*args)
    return result[0] if single else result


def planes(low, high, width, fn):
    width = min(width, high - low)

    def step(i, carry):
        fn(pl.ds(jnp.minimum(low + i * width, high - width), width))
        return carry

    lax.fori_loop(0, -(-(high - low) // width), step, 0)


def width(steps):
    return max(1, 24 // steps)


def moved(at, by):
    return pl.ds(at.start + by, at.size)


def masks():
    lane = lax.broadcasted_iota(jnp.int32, (8, 128), 1)
    row = lax.broadcasted_iota(jnp.int32, (8, 128), 0)
    y = lane % SIDE
    return y != SIDE - 1, y != 0, lane < 96, lane >= 32, row < 7, row > 0


def beside(p, m):
    shape = p.shape
    p = p.reshape((-1,) + shape[-2:])
    y_up, y_down, x_in, x_out, row_up, row_down = [jnp.broadcast_to(a[None], p.shape) for a in m]
    zero = jnp.zeros_like(p)
    up = pltpu.roll(p, 96, 2)
    down = pltpu.roll(p, 32, 2)
    total = jnp.where(y_up, pltpu.roll(p, 127, 2), zero) + jnp.where(y_down, pltpu.roll(p, 1, 2), zero)
    total = total + jnp.where(x_in, up, jnp.where(row_up, pltpu.roll(up, 7, 1), zero))
    total = total + jnp.where(x_out, down, jnp.where(row_down, pltpu.roll(down, 1, 1), zero))
    return total.reshape(shape)


def spread(ref, t0, t1, z, m):
    p = ref[t0:t1, z]
    return p, beside(p, m) + ref[t0:t1, moved(z, -1)] + ref[t0:t1, moved(z, 1)]


def turn_in(ref, store):
    for s in range(8):
        store(s, ref[s * 128 : (s + 1) * 128, :].T)


def turn_out(ref, out):
    for s in range(8):
        out[s * 128 : (s + 1) * 128, :] = ref[:, s, :].T


def share_edges(odd, ref, edge_a, edge_b):
    n = edge_a.shape[1]
    far = OWN - n
    edge_a[...] = ref[:, pl.ds(far * (1 - odd), n)]
    edge_b[...] = ref[:, pl.ds(far * odd, n)]


def step_over(odd, src, row, edge_a, edge_b, edge_row, fn):
    m = masks()
    t = slice(row, row + 1)
    a = edge_a[edge_row : edge_row + 1]
    b = edge_b[edge_row : edge_row + 1]
    low = jnp.where(odd > 0, a, b)
    high = jnp.where(odd > 0, b, a)
    p = src[t, 0:1]
    fn(pl.ds(0, 1), p, beside(p, m) + low + src[t, 1:2])
    p = src[t, OWN - 1 : OWN]
    fn(pl.ds(OWN - 1, 1), p, beside(p, m) + high + src[t, OWN - 2 : OWN - 1])
    planes(1, OWN - 1, 18, lambda z: fn(z, *spread(src, row, row + 1, z, m)))


def swept(fixed, step, z, p, near, before):
    g = fixed[step : step + 1, z]
    return keep * p + fixed[3, z] * (g + base_coef * before[0:1, z] + fixed[2, z] * near)


def left(fixed, step, z, p, near, before):
    d = fixed[2, z]
    known = fixed[step : step + 1, z] + base_coef * before[0:1, z] + d * near
    return known - (base_coef + 6.0 * d) * p


def sweep_late(flag, fixed, x, x_a, x_b, y1, out_a, out_b):
    odd = flag[0]

    def fn(z, p, near):
        y1[:, z] = swept(fixed, 1, z, p, near, x)

    step_over(odd, x, 1, x_a, x_b, 1, fn)
    share_edges(odd, y1, out_a, out_b)


def sweep_both(flag, fixed, x, x_a, x_b, prev, y1, y1_a, y1_b, y0, z1, out_a, out_b):
    odd = flag[0]

    def early(z, p, near):
        y0[:, z] = swept(fixed, 0, z, p, near, prev)

    step_over(odd, x, 0, x_a, x_b, 0, early)

    def late(z, p, near):
        z1[:, z] = swept(fixed, 1, z, p, near, y0)

    step_over(odd, y1, 0, y1_a, y1_b, 0, late)
    share_edges(odd, y0, out_a.at[0:1], out_b.at[0:1])
    share_edges(odd, z1, out_a.at[1:2], out_b.at[1:2])


def sweep_both_raw(flag, fixed, x, x_a, x_b, back, y1, y1_a, y1_b, y0, z1, out_a, out_b, prev):
    def store(s, block):
        prev[0, :, s, :] = block

    turn_in(back.at[0], store)
    sweep_both(flag, fixed, x, x_a, x_b, prev, y1, y1_a, y1_b, y0, z1, out_a, out_b)


def sweep_early(flag, fixed, y0, y_a, y_b, prev, z0, out_a, out_b):
    odd = flag[0]

    def fn(z, p, near):
        z0[:, z] = swept(fixed, 0, z, p, near, prev)

    step_over(odd, y0, 0, y_a, y_b, 0, fn)
    share_edges(odd, z0, out_a, out_b)


def turned(flag, v_ref, g_ref, d_ref, v0, fixed, edge_a, edge_b):
    def into(ref, row):
        def store(s, block):
            ref[row, :, s, :] = block

        return store

    for t in range(2):
        turn_in(v_ref.at[t], into(v0, t))
    share_edges(flag[0], v0, edge_a, edge_b)
    for t in range(2):
        turn_in(g_ref.at[t], into(fixed, t))
    turn_in(d_ref, into(fixed, 2))

    def scale(z):
        fixed[3, z] = damping / (base_coef + 6.0 * fixed[2, z])

    planes(0, OWN, 8, scale)


def restrict_left(flag, fixed, z0, z1, e0a, e0b, e1a, e1b, prev, out, out_a, out_b, held):
    odd = flag[0]

    def early(z, p, near):
        out[:, z] += 0.5 * left(fixed, 0, z, p, near, prev)

    def late(z, p, near):
        out[:, z] = 0.5 * left(fixed, 1, z, p, near, z0)

    step_over(odd, z1, 0, e1a, e1b, 1, late)
    step_over(odd, z0, 0, e0a, e0b, 0, early)
    share_edges(odd, out, out_a.at[0:1], out_b.at[0:1])
    share_edges(odd, fixed.at[2:3], out_a.at[1:2], out_b.at[1:2])
    held[0:1, 0:1] = e0a[...]
    held[1:2, 0:1] = e1a[1:2]
    held[0:1, OWN + 1 :] = e0b[...]
    held[1:2, OWN + 1 :] = e1b[1:2]

    def hold(z):
        held[0:1, moved(z, 1)] = z0[:, z]
        held[1:2, moved(z, 1)] = z1[:, z]

    planes(0, OWN, 8, hold)


def cut(flag, own, fixed, edge_a, edge_b, pieces, d_piece, tall):
    odd = flag[0]
    end = OWN + HALO
    tall[:, pl.ds(end * (1 - odd), HALO)] = edge_a[...]
    tall[:, pl.ds(end * odd, HALO)] = edge_b[...]

    def copy(z):
        tall[0:1, moved(z, HALO)] = own[:, z]
        tall[1:2, moved(z, HALO)] = fixed[2:3, z]

    planes(0, OWN, 8, copy)
    for i in range(GROUP):
        pieces[i] = tall[0, i * PIECE : i * PIECE + WIDE]
    d_piece[...] = tall[1, pl.ds(flag[1], WIDE)]


def corrected_late(flag, fixed, held, e, e_a, e_b, x, x_a, x_b, y1, out_a, out_b):
    def add(z):
        x[:, z] = held[:, moved(z, 1)] + e[:, z]

    planes(0, OWN, 8, add)
    x_a[...] = held[:, 0:1] + e_a[...]
    x_b[...] = held[:, OWN + 1 :] + e_b[...]
    sweep_late(flag, fixed, x, x_a, x_b, y1, out_a, out_b)


def corrected_both(
    flag, fixed, x, x_a, x_b, prev, e_prev, y1, y1_a, y1_b, y0, z1, out_a, out_b, total
):
    def add(z):
        total[:, z] = prev[:, z] + e_prev[:, z]

    planes(0, OWN, 8, add)
    sweep_both(flag, fixed, x, x_a, x_b, total, y1, y1_a, y1_b, y0, z1, out_a, out_b)


def finish_late(flag, fixed, z0, z1, e1a, e1b, sol_out, res):
    turn_out(z0.at[0], sol_out.at[0])
    turn_out(z1.at[0], sol_out.at[1])

    def late(z, p, near):
        res[:, z] = left(fixed, 1, z, p, near, z0)

    step_over(flag[0], z1, 0, e1a, e1b, 1, late)


def finish_early(flag, fixed, z0, e0a, e0b, prev, late, res_out, res):
    turn_out(late.at[0], res_out.at[1])

    def early(z, p, near):
        res[:, z] = left(fixed, 0, z, p, near, prev)

    step_over(flag[0], z0, 0, e0a, e0b, 0, early)
    turn_out(res.at[0], res_out.at[0])


def step_alone(d_ref, g_own, v2, below, tail, s_ref, va, *, c):
    n = g_own.shape[0]
    m = masks()

    def gather(z):
        s = damping / (c + 6.0 * d_ref[z])
        s_ref[z] = s
        va[:, z] = s * g_own[:, z]

    planes(0, WIDE, width(n), gather)

    def sweep(z):
        p, near = spread(va, 1, n, z, m)
        v2[:, moved(z, -1)] = keep * p + s_ref[z] * (
            g_own[1:n, z] + c * va[0 : n - 1, z] + d_ref[z] * near
        )

    planes(1, WIDE - 1, width(n - 1), sweep)

    def left(z):
        zz = moved(z, -1)
        p, near = spread(v2, 1, n - 1, zz, m)
        d = d_ref[z]
        r = g_own[2:n, z] + c * v2[0 : n - 2, zz] + d * near - (c + 6.0 * d) * p
        for j in range(n // 2 - 1):
            value = 0.5 * (r[2 * j] + r[2 * j + 1])
            below[j, moved(z, -2)] = value
            if j >= n // 2 - 3:
                tail[j - n // 2 + 3, moved(z, -2)] = value

    planes(2, WIDE - 2, width(n - 2), left)


def step_join(flag, d_ref, history, g_own, v2, first, below, kept, s_ref, g_ref, va, vb, *, c, keep_low):
    known = jnp.where(flag[0] > 0, 1.0, 0.0).astype(F32)
    m = masks()

    def gather(z):
        s = damping / (c + 6.0 * d_ref[z])
        s_ref[z] = s
        g = known * history[:, z]
        g_ref[0:2, z] = g
        va[0:2, z] = s * g
        g = g_own[0:1, z]
        g_ref[2:3, z] = g
        va[2:3, z] = s * g

    planes(0, WIDE, 8, gather)

    def sweep(z):
        p, near = spread(va, 1, 3, z, m)
        value = keep * p + s_ref[z] * (g_ref[1:3, z] + c * va[0:2, z] + d_ref[z] * near)
        vb[0:2, z] = value
        vb[2, z] = v2[0, moved(z, -1)]
        first[:, moved(z, -1)] = value[1:2]

    planes(1, WIDE - 1, 10, sweep)

    def left(z):
        p, near = spread(vb, 1, 3, z, m)
        d = d_ref[z]
        r = g_own[0:2, z] + c * vb[0:2, z] + d * near - (c + 6.0 * d) * p
        below[0, moved(z, -2)] = 0.5 * (r[0] + r[1])

    planes(2, WIDE - 2, 10, left)
    kept[0:1] = g_ref[1:2, keep_low : WIDE - keep_low]
    kept[1:] = g_own[:, keep_low : WIDE - keep_low]


def step_down(flag, d_ref, *refs, parts, c, low, last, keep_low):
    arrays = refs[: len(parts)]
    rest = refs[len(parts) :]
    past = sum(n for n, need in parts if need)
    total = sum(n for n, need in parts)
    own = total - past
    high = WIDE - low
    q = flag[0]
    if last:
        v_above, e_ref, tail, s_ref, g_ref, va, vb = rest
    else:
        v2, below, kept, s_ref, g_ref, va = rest

    def gather(z):
        s = damping / (c + 6.0 * d_ref[z])
        s_ref[z] = s
        at = 0
        for ref, (n, need) in zip(arrays, parts):
            g = ref[:, moved(z, -low)]
            if need:
                g = jnp.where(q >= need, 1.0, 0.0).astype(F32) * g
            g_ref[at : at + n, z] = g
            va[at : at + n, z] = s * g
            at += n

    planes(low, high, width(total), gather)
    m = masks()

    def sweep(src, start, margin, store):
        def fn(z):
            p, near = spread(src, start, total, z, m)
            value = keep * p + s_ref[z] * (
                g_ref[start:total, z] + c * src[start - 1 : total - 1, z] + d_ref[z] * near
            )
            store(z, value)

        planes(low + margin, high - margin, width(total - start), fn)

    if last:

        def keep_b(z, value):
            vb[1:total, z] = value

        def keep_a(z, value):
            va[2:total, z] = value

        def keep_e(z, value):
            e_ref[:, moved(z, -low - 3)] = value
            tail[:, moved(z, -low - 3)] = v_above[v_above.shape[0] - 2 :, moved(z, 1 - low)] + value

        sweep(va, 1, 1, keep_b)
        sweep(vb, 2, 2, keep_a)
        sweep(va, 3, 3, keep_e)
        return

    def keep_v(z, value):
        v2[:, moved(z, -low - 1)] = value

    sweep(va, 1, 1, keep_v)

    def left(z):
        zz = moved(z, -low - 1)
        p, near = spread(v2, past - 1, total - 1, zz, m)
        d = d_ref[z]
        r = g_ref[past:total, z] + c * v2[past - 2 : total - 2, zz] + d * near - (c + 6.0 * d) * p
        for j in range(own // 2):
            below[j, moved(z, -low - 2)] = 0.5 * (r[2 * j] + r[2 * j + 1])

    planes(low + 2, high - 2, width(own), left)
    kept[...] = g_ref[past - 1 :, keep_low : WIDE - keep_low]


def step_up(flag, d_ref, kept, v_last, e_own, *refs, firsts, own, c, low, e_low, top):
    values = refs[: len(firsts)]
    if top:
        out, s_ref, va, vb = refs[len(firsts) :]
    else:
        v_above, out, tail, s_ref, va, vb = refs[len(firsts) :]
    known = jnp.where(flag[0] > 0, 1.0, 0.0).astype(F32)
    n = own + 2

    def correct(z):
        s_ref[z] = damping / (c + 6.0 * d_ref[z])
        zz = moved(z, -low - 1)
        here = moved(z, -e_low)
        va[0:2, z] = known * v_last[:, here]
        for step in range(own):
            ref, first = [(r, f) for r, f in zip(values, firsts) if f <= step][-1]
            va[2 + step, z] = ref[step - first, zz] + e_own[step // 2, here]

    planes(e_low, WIDE - e_low, width(n), correct)
    m = masks()

    def sweep1(z):
        p, near = spread(va, 1, n, z, m)
        g = kept[:, moved(z, -e_low - 1)]
        vb[:, z] = keep * p + s_ref[z] * (g + c * va[0 : n - 1, z] + d_ref[z] * near)

    planes(e_low + 1, WIDE - e_low - 1, width(n - 1), sweep1)

    def sweep2(z):
        p, near = spread(vb, 1, n - 1, z, m)
        g = kept[1:, moved(z, -e_low - 1)]
        value = keep * p + s_ref[z] * (g + c * vb[0 : n - 2, z] + d_ref[z] * near)
        here = moved(z, -e_low - 2)
        out[:, here] = value
        if not top:
            tail[:, here] = v_above[v_above.shape[0] - 2 :, moved(z, 1 - low)] + value[own - 1 :]

    planes(e_low + 2, WIDE - e_low - 2, width(own), sweep2)


def later(block, distance):
    count = lax.axis_size("tm")
    return lax.ppermute(block, "tm", [(i, i + distance) for i in range(count - distance)])


def around(block, distance):
    count = lax.axis_size("tm")
    return lax.ppermute(block, "tm", [(i, (i + distance) % count) for i in range(count)])


def body(source, initial_guess, diffusivity):
    T = (8, 128)
    slabs = lax.axis_size("gz")
    count = lax.axis_size("tm")
    odd = (lax.axis_index("gz") % 2).astype(jnp.int32).reshape(1)
    me = lax.axis_index("tm").astype(jnp.int32)
    q = (me // GROUP).reshape(1)
    piece = jnp.concatenate([odd, (me % GROUP * PIECE).reshape(1)])
    pairs = [(i, i + 1) for i in range(1, slabs - 1, 2)]
    pairs = pairs + [(b, a) for a, b in pairs]

    def swapped(edge_a, edge_b):
        return (
            lax.ppermute(edge_a, "gz", [(i, i ^ 1) for i in range(slabs)]),
            lax.ppermute(edge_b, "gz", pairs),
        )

    flat = lambda a: a.reshape(a.shape[:-3] + (SIDE * SIDE, OWN))
    guess = flat(initial_guess)
    prev = later(guess[1:2], 1)
    plane = (1, OWN) + T
    edge = [(1, 1) + T] * 2
    edges = [(2, 1) + T] * 2
    run = functools.partial(call, n_scalar=1)
    x, fixed, *ends = run(
        turned,
        [(2, OWN) + T, (4, OWN) + T] + edges,
        (odd, guess, flat(source), flat(diffusivity)),
    )
    x = (x, *swapped(*ends))
    y1, *ends = run(sweep_late, [plane] + edge, (odd, fixed, *x))
    y1_prev = later(y1, 1)
    y0, z1, *ends = run(
        sweep_both_raw,
        [plane, plane] + edges,
        (odd, fixed, *x, prev, y1, *swapped(*ends)),
        scratch=[plane],
    )
    v2_prev = later(z1, 1)
    late_ends = swapped(*ends)
    z0, *ends = run(sweep_early, [plane] + edge, (odd, fixed, y0, *late_ends, y1_prev))
    g1, *ends, held = run(
        restrict_left,
        [plane] + [(2, HALO) + T] * 2 + [(2, OWN + 2) + T],
        (odd, fixed, z0, z1, *swapped(*ends), *late_ends, v2_prev),
    )
    pieces, d = call(
        cut,
        [(GROUP, WIDE) + T, (WIDE,) + T],
        (piece, g1, fixed, *swapped(*ends)),
        scratch=[(2, OWN + 2 * HALO) + T],
        n_scalar=1,
    )
    groups = [list(range(a, a + GROUP)) for a in range(0, count, GROUP)]
    g = lax.all_to_all(pieces, "tm", 0, 0, axis_index_groups=groups, tiled=True)

    c = base_coef / 2.0
    history = around(g[-2:], GROUP)
    n = GROUP
    v, g_rest, g_tail = call(
        functools.partial(step_alone, c=c),
        [(n - 1, WIDE - 2) + T, (n // 2 - 1, WIDE - 4) + T, (2, WIDE - 4) + T],
        (d, g),
        scratch=[(WIDE,) + T, (n, WIDE) + T],
    )
    next_history = around(g_tail, GROUP)
    first, g_first, kept = run(
        functools.partial(step_join, c=c, keep_low=14),
        [(1, WIDE - 2) + T, (1, WIDE - 4) + T, (n + 1, WIDE - 28) + T],
        (q, d, history, g, v),
        scratch=[(WIDE,) + T] + [(3, WIDE) + T] * 3,
    )
    saved = [((first, v), (0, 1), kept, n, c, 0)]
    parts = [(2, 1), (1, 0), (3, 0)]
    arrays = [next_history, g_first, g_rest]
    for level in (2, 3):
        n, c, low = n // 2, c / 2.0, 2 * level - 2
        wide = WIDE - 2 * low
        keep_low = 16 - 2 * level
        v, g, kept = run(
            functools.partial(
                step_down, parts=parts, c=c, low=low, last=False, keep_low=keep_low
            ),
            [(n + 1, wide - 2) + T, (n // 2, wide - 4) + T, (n + 1, WIDE - 2 * keep_low) + T],
            (q, d, *arrays),
            scratch=[(WIDE,) + T, (n + 2, WIDE) + T, (n + 2, WIDE) + T],
        )
        saved.append(((v,), (-1,), kept, n, c, low))
        if level == 2:
            parts = [(2, 1), (2, 0)]
            arrays = [around(g, GROUP), g]
    parts = [(1, 3), (1, 2), (1, 1), (1, 0)]
    arrays = [around(g, i * GROUP) for i in (3, 2, 1)] + [g]
    low = 6
    wide = WIDE - 2 * low
    e, tail = run(
        functools.partial(step_down, parts=parts, c=c / 2.0, low=low, last=True, keep_low=0),
        [(1, wide - 6) + T, (2, wide - 6) + T],
        (q, d, *arrays, saved[-1][0][-1]),
        scratch=[(WIDE,) + T] + [(4, WIDE) + T] * 3,
    )
    e_low = low + 3
    while saved:
        values, firsts, kept, n, c, low = saved.pop()
        v_last = around(tail, GROUP)
        top = not saved
        narrow = WIDE - 2 * e_low - 4
        e, *tail = run(
            functools.partial(
                step_up, firsts=firsts, own=n, c=c, low=low, e_low=e_low, top=top
            ),
            [(n, narrow) + T] + [(2, narrow) + T] * (not top),
            (q, d, kept, v_last, e, *values) + (() if top else (saved[-1][0][-1],)),
            scratch=[(WIDE,) + T, (n + 2, WIDE) + T, (n + 1, WIDE) + T],
        )
        tail = tail[0] if tail else None
        e_low += 2
    e0 = lax.all_to_all(e, "tm", 0, 0, axis_index_groups=groups, tiled=True)
    e0 = e0.reshape((1, OWN) + T)
    e_prev = later(e0, 1)
    side = (OWN - 1) * (1 - odd[0])
    e_a = lax.dynamic_slice_in_dim(e0, side, 1, axis=1)
    e_b = lax.dynamic_slice_in_dim(e0, OWN - 1 - side, 1, axis=1)
    *x, y1, out_a, out_b = run(
        corrected_late,
        [(2, OWN) + T] + edges + [plane] + edge,
        (odd, fixed, held, e0, *swapped(e_a, e_b)),
    )
    y1_prev = later(y1, 1)
    y0, z1, *ends = run(
        corrected_both,
        [plane, plane] + edges,
        (odd, fixed, *x, v2_prev, e_prev, y1, *swapped(out_a, out_b)),
        scratch=[plane],
    )
    prev = later(z1, 1)
    late_ends = swapped(*ends)
    z0, *ends = run(sweep_early, [plane] + edge, (odd, fixed, y0, *late_ends, y1_prev))
    sol, res = run(
        finish_late, [(2, SIDE * SIDE, OWN), plane], (odd, fixed, z0, z1, *late_ends)
    )
    res = run(
        finish_early,
        (2, SIDE * SIDE, OWN),
        (odd, fixed, z0, *swapped(*ends), prev, res),
        scratch=[plane],
    )
    return sol.reshape(source.shape), res.reshape(source.shape)


def solution(mesh):
    placed = (P("tm", None, None, "gz"), P("tm", None, None, "gz"), P(None, None, "gz"))
    return jax.shard_map(
        body,
        mesh=mesh,
        in_specs=placed,
        out_specs=(P("tm", None, None, "gz"), P("tm", None, None, "gz")),
        check_vma=False,
    )
```
